32 devices in a mesh: dp: 8 (over z, y), mp: 4 (over x, core).
Axes of the slice: x: 2, y: 2, z: 4, core: 2. Of those that a mesh axis runs over, the one named last changes fastest.
Arguments:
- inputs: bfloat16 [12608, 768], P('dp'), may hold values from -6 to 6
- cotangent: float32 [12608, 768], P('dp'), may hold values from -6 to 6
- ln_gain: float32 [2, 2, 768], replicated, may hold values from 0.1 to 1.9
- ln_bias: float32 [2, 2, 768], replicated, may hold values from -3 to 3
- w_qkv: bfloat16 [2, 768, 3, 768], P(None, 'dp', None, 'mp'), may hold values from -0.21875 to 0.21875
- b_qv: float32 [2, 2, 768], P(None, None, 'mp'), may hold values from -3 to 3
- w_out: bfloat16 [2, 768, 768], P(None, 'dp', 'mp'), may hold values from -0.875 to 0.875
- b_out: float32 [2, 768], replicated, may hold values from -3 to 3
- w_fc1: bfloat16 [768, 3072], P('dp', 'mp'), may hold values from -0.21875 to 0.21875
- b_fc1: float32 [3072], P('mp'), may hold values from -3 to 3
- w_fc2: bfloat16 [768, 3072], P('dp', 'mp'), may hold values from -0.109375 to 0.109375
- b_fc2: float32 [768], replicated, may hold values from -3 to 3
- w_gate: bfloat16 [768, 8], P('dp'), may hold values from -0.109375 to 0.109375
- e_in: bfloat16 [8, 768, 3072], P('dp', None, 'mp'), may hold values from -0.21875 to 0.21875
- e_in_bias: float32 [8, 3072], P('dp', 'mp'), may hold values from -3 to 3
- e_out: bfloat16 [8, 768, 3072], P('dp', None, 'mp'), may hold values from -0.4375 to 0.4375
- e_out_bias: float32 [8, 768], P('dp'), may hold values from -6 to 6
- routes: int32 [12608, 2], P('dp'), may hold values from 0 to 7, all different within a row; in each aligned block of 788 rows (0 to 787, 788 to 1575, ...) at most 248 rows name the same one
Outputs:
- outputs: bfloat16 [12608, 768], P('dp')
- grad_inputs: float32 [12608, 768], P('dp')
- grad_ln_gain: float32 [2, 2, 768], replicated
- grad_ln_bias: float32 [2, 2, 768], replicated
- grad_w_qkv: float32 [2, 768, 3, 768], P(None, 'dp', None, 'mp')
- grad_b_qv: float32 [2, 2, 768], P(None, None, 'mp')
- grad_w_out: float32 [2, 768, 768], P(None, 'dp', 'mp')
- grad_b_out: float32 [2, 768], replicated
- grad_w_fc1: float32 [768, 3072], P('dp', 'mp')
- grad_b_fc1: float32 [3072], P('mp')
- grad_w_fc2: float32 [768, 3072], P('dp', 'mp')
- grad_b_fc2: float32 [768], replicated
- grad_w_gate: float32 [768, 8], P('dp')
- grad_e_in: float32 [8, 768, 3072], P('dp', None, 'mp')
- grad_e_in_bias: float32 [8, 3072], P('dp', 'mp')
- grad_e_out: float32 [8, 768, 3072], P('dp', None, 'mp')
- grad_e_out_bias: float32 [8, 768], P('dp')
The draws below stay inside these ranges and needn't reach their ends.
Inputs may be any that keep to these rules, and one draw needn't show every extreme that they name: `routes`: in each aligned block of 788 rows (one micro-batch of one dp index) no expert is named by more than 248 rows; the 2 experts of a row differ.
All inputs are finite; a program needn't handle non-finite values.
Results may differ from the reference program's by a relative error of at most 0.017.
Values may be sent and summed in bfloat16 or wider, within the bound.
No kernel may reach another device: no remote copies, remote signals or barrier semaphores. Data moves between devices by JAX's collectives and lax.ppermute only.
A program may use at most 320 MiB of HBM per device.

```python
import math
import jax
import jax.numpy as jnp
import numpy as np
from jax import lax

D = 768
HEADS = 12
MLP = 3072
EXP_HID = 3072
TOP = 2
SEQ = 197
HEAD_DIM = 64
EXPERTS = 8
MB_TOK = 788
TOKENS = 12608
CAP = 248


def level_of(key, extent, shards, least, high):
    gain, own = 1.0, jax.random.fold_in(key, 6)
    for position, shards_of in shards:
        draws = jnp.exp(jax.random.uniform(jax.random.fold_in(own, position), (shards_of,), jnp.float32, least / len(shards), high / len(shards)))
        gain = gain * jnp.repeat(draws, extent[position] // shards_of).reshape([-1 if axis == position else 1 for axis in range(len(extent))])
    return gain


def deal_out(key, own, number, rows, amount, top, most, skew):
    sequence = jax.random.permutation(key, amount)
    heavy_load, ordinary = shares(amount, rows * top, most, skew, True), shares(amount, rows * top, most, skew, False)
    places = jnp.arange(amount)

    def named(sizes, rotation):
        used = int((sizes > 0).sum())
        fixed = max(1, used // 4)
        moved = fixed + (places - fixed + rotation * (used - fixed)) % max(1, amount - fixed)
        return jnp.zeros((amount,), jnp.int32).at[sequence[jnp.where(places < fixed, places, moved)]].set(jnp.asarray(sizes, jnp.int32))

    sizes = jnp.where(number % 4 == 0, named(heavy_load, number // 4), named(ordinary, number - number // 4 - 1))
    mixed = jax.random.permutation(jax.random.fold_in(own, 3), amount)
    giver, taker = mixed[0:amount // 2 * 2:2], mixed[1:amount // 2 * 2:2]
    room = jnp.minimum(sizes[giver] - 1, most - sizes[taker]) // 2
    room = jnp.where((giver == sequence[0]) | (taker == sequence[0]) | (sizes[taker] == 0), 0, jnp.maximum(room, 0))
    moved = jax.random.randint(jax.random.fold_in(own, 4), (amount // 2,), 0, 1 << 20) % (room + 1)
    sizes = sizes.at[giver].add(-moved).at[taker].add(moved)
    items = jnp.searchsorted(jnp.cumsum(sizes), jnp.arange(rows * top), side="right").astype(jnp.int32)
    grid = items.reshape(top, rows).T
    grid = grid[jax.random.permutation(jax.random.fold_in(own, 1), rows)]
    rotation = jax.random.randint(jax.random.fold_in(own, 2), (rows, 1), 0, top)
    return jnp.take_along_axis(grid, (jnp.arange(top)[None, :] + rotation) % top, axis=1)


def shares(count, total, reach, skew, full):
    loads = [(1 << 20) // math.isqrt(rank ** skew) + 1 for rank in range(1, count + 1)]
    largest = reach if full else min(reach, max(-(-total // count), total * loads[0] // sum(loads)))
    least = 1 if total - largest >= count - 1 else 0
    holding, spare = [largest] + [least] * (count - 1), total - largest - least * (count - 1)
    while spare > 0:
        free = [i for i in range(1, count) if holding[i] < largest] or [i for i in range(1, count) if holding[i] < reach]
        pool, budget = sum([loads[i] for i in free]), spare
        for i in free:
            extra = min(reach - holding[i], max(1, budget * loads[i] // pool), spare)
            holding[i] = holding[i] + extra
            spare = spare - extra
    return np.array(holding)


def scatter_about(key, shape, spread, most, shards=(), held_as=jnp.bfloat16):
    values = jax.random.normal(key, shape, jnp.float32) * spread
    if len(shards) > 0:
        values = level_of(key, shape, shards, -0.22, 0.18) * values
    return jnp.clip(values, min=-most, max=most).astype(held_as)


def setup_inputs(seed: int = 0) -> dict:
    seeds = jax.random.split(jax.random.key(seed), 19)
    inputs = scatter_about(seeds[0], (TOKENS, D), 1.0, 6.0, ((0, 8),))
    cotangent = scatter_about(seeds[1], (TOKENS, D), 1.0, 6.0, ((0, 8),), jnp.float32)
    ln_gain = jnp.clip(1.0 + 0.18 * jax.random.normal(seeds[2], (2, 2, D), jnp.float32), 0.1, 1.9)
    ln_bias = scatter_about(seeds[3], (2, 2, D), 0.5, 3.0, (), jnp.float32)
    w_qkv = scatter_about(seeds[4], (2, D, 3, D), D ** -0.5, 0.21875, ((1, 8), (3, 4)))
    b_qv = scatter_about(seeds[5], (2, 2, D), 0.5, 3.0, ((2, 4),), jnp.float32)
    w_out = scatter_about(seeds[6], (2, D, D), (D // 16) ** -0.5, 0.875, ((1, 8), (2, 4)))
    b_out = scatter_about(seeds[7], (2, D), 0.5, 3.0, (), jnp.float32)
    w_fc1 = scatter_about(seeds[8], (D, MLP), D ** -0.5, 0.21875, ((0, 8), (1, 4)))
    b_fc1 = scatter_about(seeds[9], (MLP,), 0.5, 3.0, ((0, 4),), jnp.float32)
    w_fc2 = scatter_about(seeds[10], (D, MLP), MLP ** -0.5, 0.109375, ((0, 8), (1, 4)))
    b_fc2 = scatter_about(seeds[11], (D,), 0.5, 3.0, (), jnp.float32)
    w_gate = scatter_about(seeds[12], (D, EXPERTS), (4 * D) ** -0.5, 0.109375, ((0, 8),))
    e_in = scatter_about(seeds[13], (EXPERTS, D, EXP_HID), D ** -0.5, 0.21875, ((0, 8), (2, 4)))
    e_in_bias = scatter_about(seeds[14], (EXPERTS, EXP_HID), 0.5, 3.0, ((0, 8), (1, 4)), jnp.float32)
    e_out = scatter_about(seeds[15], (EXPERTS, D, EXP_HID), (max(EXP_HID // 16, 1)) ** -0.5, 0.4375, ((0, 8), (2, 4)))
    e_out_bias = scatter_about(seeds[16], (EXPERTS, D), 1.0, 6.0, ((0, 8),), jnp.float32)
    routes_keys = jax.random.split(jax.random.fold_in(seeds[17], 1), TOKENS // MB_TOK)
    routes_turns = jax.random.permutation(jax.random.fold_in(seeds[17], 3), TOKENS // MB_TOK)
    routes = jax.vmap(lambda own, number: deal_out(jax.random.fold_in(seeds[17], 2), own, number, MB_TOK, EXPERTS, TOP, CAP, 1))(routes_keys, routes_turns).reshape((TOKENS, TOP))
    return {"inputs": inputs, "cotangent": cotangent, "ln_gain": ln_gain, "ln_bias": ln_bias, "w_qkv": w_qkv, "b_qv": b_qv, "w_out": w_out, "b_out": b_out, "w_fc1": w_fc1, "b_fc1": b_fc1, "w_fc2": w_fc2, "b_fc2": b_fc2, "w_gate": w_gate, "e_in": e_in, "e_in_bias": e_in_bias, "e_out": e_out, "e_out_bias": e_out_bias, "routes": routes}


@jax.custom_vjp
def low(v):
    return lax.optimization_barrier(v.astype(jnp.bfloat16)).astype(jnp.float32)

@jax.custom_vjp
def low_back(v):
    return v

def low_keep(v):
    return (low(v), None)

def low_pass(kept, grad):
    return (grad,)

def back_keep(v):
    return (v, None)

def back_low(kept, grad):
    return (low(grad),)
low.defvjp(low_keep, low_pass)
low_back.defvjp(back_keep, back_low)
EPSILON = 1e-06
MASKED = -1e+30
PRECISE = lax.Precision.HIGHEST

def layer_norm(hidden, norm_gain, norm_shift):
    row_mean = lax.optimization_barrier(jnp.mean(hidden, axis=-1, keepdims=True))
    centred = hidden - row_mean
    return centred * lax.rsqrt(lax.optimization_barrier(jnp.mean(centred * centred, axis=-1, keepdims=True)) + EPSILON) * norm_gain + norm_shift

def attend_block(parts):
    queries, key_rows, value_rows = parts
    scores = low_back(jnp.einsum('thd,shd->hts', queries, key_rows, precision=PRECISE) * HEAD_DIM ** (-0.5))
    seq_ids = jnp.arange(MB_TOK, dtype=jnp.int32) // SEQ
    same_seq = seq_ids[:, None] == seq_ids[None, :]
    scores = jnp.where(same_seq[None], scores, MASKED)
    probs_low = low(jax.nn.softmax(scores, axis=-1))
    return jnp.einsum('hts,shd->thd', probs_low, value_rows, precision=PRECISE)

def attention(hidden, layer, ln_gain, ln_bias, w_qkv, b_qv, w_out, b_out):
    normed = low(layer_norm(hidden, ln_gain[layer, 0], ln_bias[layer, 0]))
    projected = jnp.einsum('td,dch->tch', normed, w_qkv[layer], precision=PRECISE)
    queries = low_back(low(projected[:, 0] + b_qv[layer, 0]))
    key_rows = low_back(low(projected[:, 1]))
    value_rows = low_back(low(projected[:, 2] + b_qv[layer, 1]))
    block_shape = (TOKENS // MB_TOK, MB_TOK, HEADS, HEAD_DIM)
    attended = lax.map(jax.checkpoint(attend_block), (queries.reshape(block_shape), key_rows.reshape(block_shape), value_rows.reshape(block_shape)))
    attended = low_back(low(attended.reshape(TOKENS, D)))
    branch = low_back(jnp.einsum('te,de->td', attended, w_out[layer], precision=PRECISE))
    return hidden + branch + b_out[layer]

def dense_mlp(hidden, ln_gain, ln_bias, w_fc1, b_fc1, w_fc2, b_fc2):
    normed = low(layer_norm(hidden, ln_gain[0, 1], ln_bias[0, 1]))
    pre_act = low_back(jnp.dot(normed, w_fc1, precision=PRECISE) + b_fc1)
    activated = low(jax.nn.gelu(pre_act, approximate=False))
    branch = low_back(jnp.einsum('tf,df->td', activated, w_fc2, precision=PRECISE))
    return hidden + branch + b_fc2

def slot_places(routes):
    blocks = TOKENS // MB_TOK
    flat_routes = routes.reshape(blocks, MB_TOK * TOP).astype(jnp.int32)
    onehot = (flat_routes[:, :, None] == jnp.arange(EXPERTS, dtype=jnp.int32)[None, None, :]).astype(jnp.int32)
    rank_ids = jnp.cumsum(onehot, axis=1) - 1
    slot_ids = lax.optimization_barrier(jnp.sum(rank_ids * onehot, axis=2))
    block_ids = jnp.arange(blocks, dtype=jnp.int32)[:, None]
    return (flat_routes * (blocks * CAP) + block_ids * CAP + slot_ids).reshape(-1).astype(jnp.int32)

def expert_apply(parts):
    buffer, weight_in, bias_in, weight_out, bias_out = parts
    pre_act = low_back(jnp.dot(buffer, weight_in, precision=PRECISE) + bias_in)
    activated = low(jax.nn.gelu(pre_act, approximate=False))
    return jnp.einsum('cf,df->cd', activated, weight_out, precision=PRECISE) + bias_out

def mixture(hidden, ln_gain, ln_bias, w_gate, e_in, e_in_bias, e_out, e_out_bias, routes, places):
    normed = low(layer_norm(hidden, ln_gain[1, 1], ln_bias[1, 1]))
    logits = low_back(jnp.dot(normed, w_gate, precision=PRECISE))
    gate_probs = jax.nn.softmax(logits, axis=-1)
    chosen = jnp.take_along_axis(gate_probs, routes.astype(jnp.int32), axis=1)
    all_rows = EXPERTS * (TOKENS // MB_TOK) * CAP
    buffer = jnp.zeros((all_rows, D), jnp.float32).at[places].add(jnp.repeat(normed, TOP, axis=0))
    buffer = low_back(buffer).reshape(EXPERTS, all_rows // EXPERTS, D)
    result = lax.map(jax.checkpoint(expert_apply), (buffer, e_in, e_in_bias, e_out, e_out_bias))
    result = low_back(low(result)).reshape(all_rows, D)
    picked = result[places].reshape(TOKENS, TOP, D)
    return hidden + lax.optimization_barrier(jnp.sum(chosen[:, :, None] * picked, axis=1))

def reference(inputs, cotangent, ln_gain, ln_bias, w_qkv, b_qv, w_out, b_out, w_fc1, b_fc1, w_fc2, b_fc2, w_gate, e_in, e_in_bias, e_out, e_out_bias, routes):
    places = slot_places(routes)

    def forward(hidden, gains, shifts, qkv_w, qv_b, out_w, out_b, fc1_w, fc1_b, fc2_w, fc2_b, gate_w, in_w, in_b, out_e, out_eb):
        hidden = attention(hidden, 0, gains, shifts, qkv_w, qv_b, out_w, out_b)
        hidden = dense_mlp(hidden, gains, shifts, fc1_w, fc1_b, fc2_w, fc2_b)
        hidden = attention(hidden, 1, gains, shifts, qkv_w, qv_b, out_w, out_b)
        return mixture(hidden, gains, shifts, gate_w, in_w, in_b, out_e, out_eb, routes, places)
    result, pullback = jax.vjp(forward, inputs.astype(jnp.float32), ln_gain.astype(jnp.float32), ln_bias.astype(jnp.float32), w_qkv.astype(jnp.float32), b_qv.astype(jnp.float32), w_out.astype(jnp.float32), b_out.astype(jnp.float32), w_fc1.astype(jnp.float32), b_fc1.astype(jnp.float32), w_fc2.astype(jnp.float32), b_fc2.astype(jnp.float32), w_gate.astype(jnp.float32), e_in.astype(jnp.float32), e_in_bias.astype(jnp.float32), e_out.astype(jnp.float32), e_out_bias.astype(jnp.float32))
    grads = pullback(cotangent.astype(jnp.float32))
    return (result.astype(jnp.bfloat16), grads[0], grads[1], grads[2], grads[3], grads[4], grads[5], grads[6], grads[7], grads[8], grads[9], grads[10], grads[11], grads[12], grads[13], grads[14], grads[15])
```

```python
import math

import jax
import jax.numpy as jnp
from jax import lax
from jax.experimental import pallas as pl
from jax.experimental.pallas import tpu as pltpu
from jax.sharding import PartitionSpec as P

SEQ = 197
HEAD_DIM = 64
MB_TOK = 788
SEQS = MB_TOK // SEQ
PADDED = 208
ROWS = SEQS * PADDED
EPSILON = 1e-06
MASKED = -1e30
ROOT_HALF = 0.7071067811865476
DENSITY = 0.3989422804014327
LOW = jnp.bfloat16
FULL = jnp.float32
VMEM_LIMIT = 56 * 1024 * 1024


def mean_of(rows):
    return jnp.mean(rows, axis=1, keepdims=True)


def normalise(hidden):
    centred = hidden - mean_of(hidden)
    inv_std = lax.rsqrt(mean_of(centred * centred) + EPSILON)
    return centred * inv_std, inv_std


def norm_step_back(grad_out, hidden, gain):
    normed, inv_std = normalise(hidden)
    scaled = grad_out * gain
    inner = scaled - mean_of(scaled) - normed * mean_of(scaled * normed)
    return inner * inv_std, jnp.sum(grad_out * normed, axis=0, keepdims=True), jnp.sum(grad_out, axis=0, keepdims=True)


def dot_nn(left, right):
    return lax.dot_general(left, right, (((1,), (0,)), ((), ())), preferred_element_type=FULL)


def dot_tn(left, right):
    return lax.dot_general(left, right, (((0,), (0,)), ((), ())), preferred_element_type=FULL)


def dot_nt(left, right):
    return lax.dot_general(left, right, (((1,), (1,)), ((), ())), preferred_element_type=FULL)


def gelu_parts(pre_act):
    cdf = 0.5 * (1.0 + lax.erf(pre_act * ROOT_HALF))
    return pre_act * cdf, cdf + pre_act * jnp.exp(-0.5 * pre_act * pre_act) * DENSITY


def wide(rows_block, width):
    return pl.BlockSpec((rows_block, width), lambda i: (i, 0))


def fixed(shape):
    return pl.BlockSpec(shape, lambda *_: (0,) * len(shape))


def view_spec(view):
    array, block, width = view
    return pl.BlockSpec((array.shape[0], width), lambda *_: (0, block))


def sds(shape, dtype):
    return jax.ShapeDtypeStruct(shape, dtype)


def call(body, name, grid, in_specs, out_specs, out_shape, scratch, flops, args):
    moved = sum(a.size * a.dtype.itemsize for a in args) + sum(
        math.prod(o.shape) * jnp.dtype(o.dtype).itemsize for o in out_shape
    )
    return pl.pallas_call(
        body,
        name=name,
        grid=grid,
        in_specs=in_specs,
        out_specs=out_specs,
        out_shape=out_shape,
        scratch_shapes=scratch,
        cost_estimate=pl.CostEstimate(flops=int(flops), bytes_accessed=int(moved), transcendentals=0),
        compiler_params=pltpu.CompilerParams(vmem_limit_bytes=VMEM_LIMIT),
    )(*args)


def enter_forward(refs):
    if len(refs) == 1:
        return refs[0][...].astype(FULL)
    last, mine, other, bias = refs
    return last[...] + (mine[...].astype(FULL) + other[...].astype(FULL)) + bias[...]


def forward_specs(entry):
    return [fixed(e.shape) if e.shape[0] == 1 else wide(PADDED, e.shape[1]) for e in entry]


def attend_forward(entry, gain, shift, packs, bias):
    width = gain.shape[1]
    span = packs[0][2] // 4
    heads = span // HEAD_DIM
    n_entry = len(entry)

    def body(*refs):
        entry_refs = refs[:n_entry]
        gain_ref, shift_ref, w0, w1, b0, b1 = refs[n_entry : n_entry + 6]
        hid_ref, low_ref, qkv_ref, lse_ref, att_ref, part_ref = refs[n_entry + 6 :]
        hidden = enter_forward(entry_refs)
        hid_ref[...] = hidden
        low = (normalise(hidden)[0] * gain_ref[...] + shift_ref[...]).astype(LOW)
        low_ref[...] = low
        inside = lax.broadcasted_iota(jnp.int32, (PADDED, PADDED), 1) < SEQ
        lanes = lax.broadcasted_iota(jnp.int32, (PADDED, 128), 1)
        lse = jnp.zeros((PADDED, 128), FULL)
        part = None
        for g, (w, b) in enumerate(((w0, b0), (w1, b1))):
            projected = dot_nn(low, w[:, : 3 * span])
            queries = (projected[:, :span] + b[0:1, :]).astype(LOW)
            keys = projected[:, span : 2 * span].astype(LOW)
            values = (projected[:, 2 * span :] + b[1:2, :]).astype(LOW)
            base = 3 * span * g
            qkv_ref[:, base : base + 3 * span] = jnp.concatenate([queries, keys, values], axis=1)
            attended = []
            for h in range(heads):
                cut = slice(h * HEAD_DIM, (h + 1) * HEAD_DIM)
                scores = dot_nt(queries[:, cut], keys[:, cut]) * HEAD_DIM**-0.5
                scores = jnp.where(inside, scores, MASKED)
                top = jnp.max(scores, axis=1, keepdims=True)
                exps = jnp.exp(scores - top)
                total = jnp.sum(exps, axis=1, keepdims=True)
                lse = jnp.where(lanes == g * heads + h, top + jnp.log(total), lse)
                probs = (exps / total).astype(LOW)
                attended.append(dot_nn(probs, values[:, cut]).astype(LOW))
            attended = jnp.concatenate(attended, axis=1)
            att_ref[:, g * span : (g + 1) * span] = attended
            branch = dot_nt(attended, w[:, 3 * span :])
            part = branch if part is None else part + branch
        lse_ref[...] = lse
        part_ref[...] = part.astype(LOW)

    rest = [gain, shift]
    args = list(entry) + rest + [packs[0][0], packs[1][0], bias[0], bias[1]]
    in_specs = forward_specs(entry) + [fixed(a.shape) for a in rest] + [view_spec(v) for v in packs]
    in_specs += [fixed(b.shape) for b in bias]
    out_shape = [
        sds((ROWS, width), FULL), sds((ROWS, width), LOW), sds((ROWS, 6 * span), LOW),
        sds((ROWS, 128), FULL), sds((ROWS, 2 * span), LOW), sds((ROWS, width), LOW),
    ]
    out_specs = [wide(PADDED, o.shape[1]) for o in out_shape]
    flops = 2 * ROWS * width * span * 8
    return call(body, "attend_forward", (SEQS,), in_specs, out_specs, out_shape, [], flops, args)


def dense_forward(entry, gain, shift, up, bias, down):
    width = gain.shape[1]
    units = up[0][2]
    n_entry = len(entry)

    def body(*refs):
        entry_refs = refs[:n_entry]
        gain_ref, shift_ref, u0, u1, b0, b1, d0, d1 = refs[n_entry : n_entry + 8]
        hid_ref, low_ref, act_ref, slope_ref, part_ref = refs[n_entry + 8 :]
        hidden = enter_forward(entry_refs)
        hid_ref[...] = hidden
        low = (normalise(hidden)[0] * gain_ref[...] + shift_ref[...]).astype(LOW)
        low_ref[...] = low
        part = None
        for g, (u, b, d) in enumerate(((u0, b0, d0), (u1, b1, d1))):
            value, slope = gelu_parts(dot_nn(low, u[...]) + b[...])
            value = value.astype(LOW)
            act_ref[:, g * units : (g + 1) * units] = value
            slope_ref[:, g * units : (g + 1) * units] = slope.astype(LOW)
            branch = dot_nt(value, d[...])
            part = branch if part is None else part + branch
        part_ref[...] = part.astype(LOW)

    rest = [gain, shift]
    args = list(entry) + rest + [up[0][0], up[1][0], bias[0], bias[1], down[0][0], down[1][0]]
    in_specs = forward_specs(entry) + [fixed(a.shape) for a in rest] + [view_spec(v) for v in up]
    in_specs += [fixed(b.shape) for b in bias] + [view_spec(v) for v in down]
    out_shape = [
        sds((ROWS, width), FULL), sds((ROWS, width), LOW), sds((ROWS, 2 * units), LOW),
        sds((ROWS, 2 * units), LOW), sds((ROWS, width), LOW),
    ]
    out_specs = [wide(PADDED, o.shape[1]) for o in out_shape]
    flops = 2 * ROWS * width * units * 4
    return call(body, "dense_forward", (SEQS,), in_specs, out_specs, out_shape, [], flops, args)


def enter_backward(grad_ref, mine_ref, other_ref, hid_ref, gain_ref, sums_ref):
    step = pl.program_id(0)
    grad_out = mine_ref[...].astype(FULL) + other_ref[...].astype(FULL)
    dx, gain_sum, shift_sum = norm_step_back(grad_out, hid_ref[...], gain_ref[...])
    grad = grad_ref[...] + dx
    sums = jnp.concatenate([gain_sum, shift_sum, jnp.sum(grad, axis=0, keepdims=True)], axis=0)

    @pl.when(step == 0)
    def _():
        sums_ref[...] = jnp.zeros_like(sums_ref)

    sums_ref[0:3, :] += sums
    return grad


def accumulate(ref, value):
    step = pl.program_id(0)

    @pl.when(step == 0)
    def _():
        ref[...] = value

    @pl.when(step > 0)
    def _():
        ref[...] += value


def attend_backward(grad, mine, other, hidden_out, gain, qkv_saved, lse, packs):
    width = gain.shape[1]
    span = packs[0][2] // 4
    heads = span // HEAD_DIM

    def body(
        grad_ref, mine_ref, other_ref, hid_ref, gain_ref, saved_ref, lse_ref, w0, w1,
        grad_out_ref, low_ref, part_ref, joined0_ref, joined1_ref, sums_ref, bias_ref,
    ):
        grad = enter_backward(grad_ref, mine_ref, other_ref, hid_ref, gain_ref, sums_ref)
        grad_out_ref[...] = grad
        grad_low = grad.astype(LOW)
        low_ref[...] = grad_low
        inside = lax.broadcasted_iota(jnp.int32, (PADDED, PADDED), 1) < SEQ
        part = None
        biases = []
        for g, (w, joined_ref) in enumerate(((w0, joined0_ref), (w1, joined1_ref))):
            grad_att = dot_nn(grad_low, w[:, 3 * span :]).astype(LOW)
            base = 3 * span * g
            queries = saved_ref[:, base : base + span]
            keys = saved_ref[:, base + span : base + 2 * span]
            values = saved_ref[:, base + 2 * span : base + 3 * span]
            dq, dk, dv = [], [], []
            for h in range(heads):
                cut = slice(h * HEAD_DIM, (h + 1) * HEAD_DIM)
                q, k, v, d = queries[:, cut], keys[:, cut], values[:, cut], grad_att[:, cut]
                scores = jnp.where(inside, dot_nt(q, k) * HEAD_DIM**-0.5, MASKED)
                place = g * heads + h
                probs = jnp.exp(scores - lse_ref[:, place : place + 1])
                dv.append(dot_tn(probs.astype(LOW), d))
                grad_probs = dot_nt(d, v)
                inner = jnp.sum(probs * grad_probs, axis=1, keepdims=True)
                grad_scores = (probs * (grad_probs - inner)).astype(LOW)
                dq.append(dot_nn(grad_scores, k) * HEAD_DIM**-0.5)
                dk.append(dot_tn(grad_scores, q) * HEAD_DIM**-0.5)
            joined = jnp.concatenate(dq + dk + dv, axis=1).astype(LOW)
            joined_ref[...] = joined
            sums = jnp.sum(joined.astype(FULL), axis=0, keepdims=True)
            biases.append(jnp.concatenate([sums, jnp.zeros((1, span), FULL)], axis=1))
            branch = dot_nt(joined, w[:, : 3 * span])
            part = branch if part is None else part + branch
        part_ref[...] = part.astype(LOW)
        biases.append(jnp.zeros((6, 4 * span), FULL))
        accumulate(bias_ref, jnp.concatenate(biases, axis=0))

    rows_args = [grad, mine, other, hidden_out, gain, qkv_saved, lse]
    args = rows_args + [packs[0][0], packs[1][0]]
    in_specs = [wide(PADDED, a.shape[1]) if a.shape[0] == ROWS else fixed(a.shape) for a in rows_args]
    in_specs += [view_spec(v) for v in packs]
    out_shape = [
        sds((ROWS, width), FULL), sds((ROWS, width), LOW), sds((ROWS, width), LOW),
        sds((ROWS, 3 * span), LOW), sds((ROWS, 3 * span), LOW),
        sds((8, width), FULL), sds((8, 4 * span), FULL),
    ]
    out_specs = [wide(PADDED, o.shape[1]) for o in out_shape[:5]] + [fixed(o.shape) for o in out_shape[5:]]
    flops = 2 * ROWS * width * span * 8
    return call(body, "attend_backward", (SEQS,), in_specs, out_specs, out_shape, [], flops, args)


def dense_backward(grad, mine, other, hidden_out, gain, slopes, up, down):
    width = gain.shape[1]
    units = up[0][2]

    def body(
        grad_ref, mine_ref, other_ref, hid_ref, gain_ref, slope_ref, u0, u1, d0, d1,
        grad_out_ref, low_ref, part_ref, pre0_ref, pre1_ref, sums_ref, bias_ref,
    ):
        grad = enter_backward(grad_ref, mine_ref, other_ref, hid_ref, gain_ref, sums_ref)
        grad_out_ref[...] = grad
        grad_low = grad.astype(LOW)
        low_ref[...] = grad_low
        part = None
        biases = []
        for g, (u, d, pre_ref) in enumerate(((u0, d0, pre0_ref), (u1, d1, pre1_ref))):
            cut = slice(g * units, (g + 1) * units)
            grad_pre = (dot_nn(grad_low, d[...]) * slope_ref[:, cut].astype(FULL)).astype(LOW)
            pre_ref[...] = grad_pre
            biases.append(jnp.sum(grad_pre.astype(FULL), axis=0, keepdims=True))
            branch = dot_nt(grad_pre, u[...])
            part = branch if part is None else part + branch
        part_ref[...] = part.astype(LOW)
        biases.append(jnp.zeros((6, units), FULL))
        accumulate(bias_ref, jnp.concatenate(biases, axis=0))

    rows_args = [grad, mine, other, hidden_out, gain, slopes]
    args = rows_args + [v[0] for v in up + down]
    in_specs = [wide(PADDED, a.shape[1]) if a.shape[0] == ROWS else fixed(a.shape) for a in rows_args]
    in_specs += [view_spec(v) for v in up + down]
    out_shape = [
        sds((ROWS, width), FULL), sds((ROWS, width), LOW), sds((ROWS, width), LOW),
        sds((ROWS, units), LOW), sds((ROWS, units), LOW),
        sds((8, width), FULL), sds((8, units), FULL),
    ]
    out_specs = [wide(PADDED, o.shape[1]) for o in out_shape[:5]] + [fixed(o.shape) for o in out_shape[5:]]
    flops = 2 * ROWS * width * units * 4
    return call(body, "dense_backward", (SEQS,), in_specs, out_specs, out_shape, [], flops, args)


def choose(piece, values):
    out = values[-1]
    for i in range(len(values) - 2, -1, -1):
        out = jnp.where(piece == i, values[i], out)
    return out


def piece_spec(i, blocks, rows):
    def index(piece, blk):
        return (0, jnp.where(piece == i, blk, jnp.where(piece < i, 0, blocks - 1)))

    return pl.BlockSpec((rows, UNIT_BLOCK), index)


UNIT_BLOCK = 256


def expert_ahead(g_rows, out_pieces):
    rows, width = g_rows.shape
    units = out_pieces[0].shape[1]
    blocks = units // UNIT_BLOCK

    def body(g_ref, w0, w1, w2, w3, out_ref):
        w = choose(pl.program_id(0), [w0[...], w1[...], w2[...], w3[...]])
        out_ref[...] = dot_nn(g_ref[...], w).astype(LOW)

    in_specs = [fixed(g_rows.shape)] + [piece_spec(i, blocks, width) for i in range(4)]
    return call(
        body, "expert_ahead", (4, blocks), in_specs,
        [pl.BlockSpec((rows, UNIT_BLOCK), lambda piece, blk: (0, piece * blocks + blk))],
        [sds((rows, 4 * units), LOW)], [], 2 * rows * width * units * 4, [g_rows] + list(out_pieces),
    )[0]


def expert_first(x_rows, g_rows, ahead, portion, in_pieces, biases, gate, out_bias, named, named_count):
    rows, width = x_rows.shape
    units = in_pieces[0].shape[1]
    blocks = units // UNIT_BLOCK
    lanes = gate[2]
    chunk = min(256, rows)

    def body(
        x_ref, g_ref, ahead_ref, w0, w1, w2, w3, bias_ref, gate_ref, ob_ref, named_ref,
        act_ref, pre_ref, dx_ref, weight_ref, log_ref, dx_acc, inner, gates,
    ):
        piece, blk = pl.program_id(0), pl.program_id(1)
        first = (piece == 0) & (blk == 0)
        last = (piece == 3) & (blk == blocks - 1)

        @pl.when(first)
        def _():
            logits = dot_nn(x_ref[...], gate_ref[...])
            live = lax.broadcasted_iota(jnp.int32, (rows, lanes), 1) < named_count
            logits = jnp.where(live, logits, MASKED)
            exps = jnp.exp(logits - jnp.max(logits, axis=1, keepdims=True))
            probs = exps / jnp.sum(exps, axis=1, keepdims=True)
            gates[...] = probs
            weight = jnp.sum(probs * named_ref[...], axis=1, keepdims=True)
            weight_ref[...] = jnp.broadcast_to(weight, weight_ref.shape)
            start = jnp.sum(g_ref[...].astype(FULL) * ob_ref[...], axis=1, keepdims=True)
            inner[...] = jnp.broadcast_to(start, inner.shape)
            dx_acc[...] = jnp.zeros_like(dx_acc)

        w = choose(piece, [w0[...], w1[...], w2[...], w3[...]])
        for r in range(rows // chunk):
            at = slice(r * chunk, (r + 1) * chunk)
            value, slope = gelu_parts(dot_nn(x_ref[at, :], w) + bias_ref[0])
            back = ahead_ref[at, :].astype(FULL)
            value = value.astype(LOW)
            act_ref[at, :] = value
            inner[at, :] += jnp.sum(value.astype(FULL) * back, axis=1, keepdims=True)
            grad_pre = (weight_ref[at, 0:1] * back * slope).astype(LOW)
            pre_ref[at, :] = grad_pre
            dx_acc[at, :] += dot_nt(grad_pre, w)

        @pl.when(last)
        def _():
            grad_log = (inner[...] * weight_ref[...] * (named_ref[...] - gates[...])).astype(LOW)
            log_ref[...] = grad_log
            dx_ref[...] = (dx_acc[...] + dot_nt(grad_log, gate_ref[...])).astype(LOW)

    args = [x_rows, g_rows, ahead] + list(in_pieces) + [biases, gate[0], out_bias, named]
    column = lambda piece, blk: (0, piece * blocks + blk)
    in_specs = [
        fixed(x_rows.shape), pl.BlockSpec((rows, width), lambda *_: (portion, 0)),
        pl.BlockSpec((rows, UNIT_BLOCK), lambda piece, blk: (portion, piece * blocks + blk)),
    ]
    in_specs += [piece_spec(i, blocks, width) for i in range(4)]
    in_specs += [
        pl.BlockSpec((1, 1, UNIT_BLOCK), lambda piece, blk: (piece, 0, blk)),
        view_spec(gate), fixed(out_bias.shape), fixed(named.shape),
    ]
    out_shape = [
        sds((rows, 4 * units), LOW), sds((rows, 4 * units), LOW), sds((rows, width), LOW),
        sds((rows, lanes), FULL), sds((rows, lanes), LOW),
    ]
    out_specs = [pl.BlockSpec((rows, UNIT_BLOCK), column)] * 2 + [fixed(o.shape) for o in out_shape[2:]]
    scratch = [pltpu.VMEM((rows, width), FULL), pltpu.VMEM((rows, lanes), FULL), pltpu.VMEM((rows, lanes), FULL)]
    flops = 2 * rows * width * units * 8
    return call(body, "expert_first", (4, blocks), in_specs, out_specs, out_shape, scratch, flops, args)


def expert_second(x_parts, g_rows, weights, logs, acts, pres, out_pieces, out_bias):
    part_rows, width = x_parts[0].shape
    rows = 2 * part_rows
    units = out_pieces[0].shape[1]
    blocks = units // UNIT_BLOCK
    lanes = logs[0].shape[1]

    def body(
        x0, x1, g_ref, c0, c1, l0, l1, a0, a1, p0, p1, w0, w1, w2, w3, ob_ref,
        y_ref, keep_ref, send_ref, bias_ref, obias_ref, gate_ref, y_acc, scaled,
    ):
        piece, blk = pl.program_id(0), pl.program_id(1)
        first = (piece == 0) & (blk == 0)
        last = (piece == 3) & (blk == blocks - 1)
        top, low = slice(0, part_rows), slice(part_rows, rows)

        @pl.when(first)
        def _():
            sums = 0.0
            for at, c in ((top, c0), (low, c1)):
                grad_y = (c[:, 0:1] * g_ref[at, :].astype(FULL)).astype(LOW)
                scaled[at, :] = grad_y
                sums = sums + jnp.sum(grad_y.astype(FULL), axis=0, keepdims=True)
            obias_ref[...] = sums
            gate_ref[...] = dot_tn(l0[...], x0[...]) + dot_tn(l1[...], x1[...])
            y_acc[...] = jnp.broadcast_to(ob_ref[...], y_acc.shape)

        w = choose(piece, [w0[...], w1[...], w2[...], w3[...]])
        sums, grad_in, grad_out = 0.0, 0.0, 0.0
        for at, x, a, p in ((top, x0, a0, p0), (low, x1, a1, p1)):
            act, pre = a[...], p[...]
            sums = sums + jnp.sum(pre.astype(FULL), axis=0, keepdims=True)
            y_acc[at, :] += dot_nt(act, w)
            grad_in = grad_in + dot_tn(x[...], pre)
            grad_out = grad_out + dot_tn(scaled[at, :], act)
        bias_ref[0] = sums

        @pl.when(piece < 2)
        def _():
            keep_ref[0, 0] = grad_in
            keep_ref[0, 1] = grad_out

        @pl.when(piece >= 2)
        def _():
            send_ref[0, 0] = grad_in.astype(LOW)
            send_ref[0, 1] = grad_out.astype(LOW)

        @pl.when(last)
        def _():
            for at, c in ((top, c0), (low, c1)):
                y_ref[at, :] = (c[:, 0:1] * y_acc[at, :]).astype(LOW)

    def keep_at(piece, blk):
        return (jnp.where(piece < 2, piece, 1), 0, 0, jnp.where(piece < 2, blk, blocks - 1))

    def send_at(piece, blk):
        return (jnp.where(piece < 2, 0, piece - 2), 0, 0, jnp.where(piece < 2, 0, blk))

    column = pl.BlockSpec((part_rows, UNIT_BLOCK), lambda piece, blk: (0, piece * blocks + blk))
    args = list(x_parts) + [g_rows] + list(weights) + list(logs) + list(acts) + list(pres)
    in_specs = [fixed(a.shape) for a in args[:7]] + [column] * 4
    in_specs += [piece_spec(i, blocks, width) for i in range(4)] + [fixed(out_bias.shape)]
    args += list(out_pieces) + [out_bias]
    out_shape = [
        sds((rows, width), LOW), sds((2, 2, width, units), FULL), sds((2, 2, width, units), LOW),
        sds((4, 1, units), FULL), sds((1, width), FULL), sds((lanes, width), FULL),
    ]
    out_specs = [
        fixed((rows, width)), pl.BlockSpec((1, 2, width, UNIT_BLOCK), keep_at),
        pl.BlockSpec((1, 2, width, UNIT_BLOCK), send_at),
        pl.BlockSpec((1, 1, UNIT_BLOCK), lambda piece, blk: (piece, 0, blk)), fixed((1, width)), fixed((lanes, width)),
    ]
    scratch = [pltpu.VMEM((rows, width), FULL), pltpu.VMEM((rows, width), LOW)]
    flops = 2 * rows * width * units * 12
    return call(body, "expert_second", (4, blocks), in_specs, out_specs, out_shape, scratch, flops, args)


def last_norm_back(grad, mine, other, hidden, gain):
    width = gain.shape[1]

    def body(grad_ref, mine_ref, other_ref, hid_ref, gain_ref, out_ref, sums_ref):
        rows = enter_backward(grad_ref, mine_ref, other_ref, hid_ref, gain_ref, sums_ref).astype(LOW)
        for s in range(SEQS):

            @pl.when(pl.program_id(0) == s)
            def _():
                out_ref[s * SEQ : (s + 1) * SEQ, :] = rows[:SEQ]

    args = [grad, mine, other, hidden, gain]
    in_specs = [wide(PADDED, a.shape[1]) if a.shape[0] == ROWS else fixed(a.shape) for a in args]
    out_shape = [sds((MB_TOK, width), LOW), sds((8, width), FULL)]
    out_specs = [fixed((MB_TOK, width)), fixed((8, width))]
    return call(body, "last_norm", (SEQS,), in_specs, out_specs, out_shape, [], 20 * ROWS * width, args)


def last_hidden(hidden, mine, other):
    width = hidden.shape[1]

    def body(hid_ref, mine_ref, other_ref, out_ref):
        rows = hid_ref[...] + (mine_ref[...].astype(FULL) + other_ref[...].astype(FULL))
        rows = rows.astype(LOW)
        for s in range(SEQS):

            @pl.when(pl.program_id(0) == s)
            def _():
                out_ref[s * SEQ : (s + 1) * SEQ, :] = rows[:SEQ]

    args = [hidden, mine, other]
    return call(
        body, "last_hidden", (SEQS,), [wide(PADDED, width)] * 3, [fixed((MB_TOK, width))],
        [sds((MB_TOK, width), LOW)], [], 4 * ROWS * width, args,
    )[0]


def make_packs(w_qkv, w_out):
    layers, rows, kinds, span = w_qkv.shape

    def body(qkv_ref, out_w_ref, *outs):
        for l in range(layers):
            parts = [qkv_ref[l, :, kind, :] for kind in range(kinds)] + [out_w_ref[l]]
            outs[l][...] = jnp.concatenate(parts, axis=1)

    return call(
        body, "make_packs", (1,), [fixed(w_qkv.shape), fixed(w_out.shape)], [fixed((rows, 4 * span))] * layers,
        [sds((rows, 4 * span), LOW)] * layers, [], 0, [w_qkv, w_out],
    )


def assemble(place, pieces):
    rows, cols = pieces[0].shape
    ring = len(pieces) // 2

    def body(place_ref, *refs):
        out_ref = refs[-1]
        z, y = place_ref[0], place_ref[1]
        for step in range(ring):
            at = lax.rem(z - step + ring, ring) * 2
            out_ref[at + y] = refs[2 * step][...]
            out_ref[at + 1 - y] = refs[2 * step + 1][...]

    whole = pl.pallas_call(
        body,
        name="assemble",
        grid_spec=pltpu.PrefetchScalarGridSpec(
            num_scalar_prefetch=1,
            grid=(1,),
            in_specs=[fixed((rows, cols))] * len(pieces),
            out_specs=fixed((2 * ring, rows, cols)),
        ),
        out_shape=sds((2 * ring, rows, cols), pieces[0].dtype),
        cost_estimate=pl.CostEstimate(flops=0, bytes_accessed=8 * ring * rows * cols, transcendentals=0),
        compiler_params=pltpu.CompilerParams(vmem_limit_bytes=VMEM_LIMIT),
    )(place, *pieces)
    return whole.reshape(2 * ring * rows, cols)


def place_rows(routes, position, experts, half, quota, room):
    def body(route_ref, pos_ref, out_ref):
        lanes = lax.broadcasted_iota(jnp.int32, (ROWS, 128), 1)
        hot = [(lanes == route_ref[:, j : j + 1]).astype(FULL) for j in range(2)]
        row = lax.broadcasted_iota(jnp.int32, (ROWS, ROWS), 0)
        col = lax.broadcasted_iota(jnp.int32, (ROWS, ROWS), 1)
        before = dot_nn((col < row).astype(FULL).astype(LOW), (hot[0] + hot[1]).astype(LOW))
        out = jnp.full((ROWS, 128), -1, jnp.int32)
        for j in range(2):
            slot = jnp.sum(hot[j] * before, axis=1, keepdims=True).astype(jnp.int32) - pos_ref[:, 0:1] * half
            route = route_ref[:, j : j + 1]
            live = (route >= 0) & (slot >= 0) & (slot < half)
            late = (slot >= quota).astype(jnp.int32)
            place = late * (experts * room) + route * room + slot - late * quota
            place = jnp.where(live, place, -1)
            out = jnp.where(lanes == j, place, out)
        out_ref[...] = out

    args = [routes, position]
    return call(
        body, "place_rows", (1,), [fixed(a.shape) for a in args], [fixed((ROWS, 128))],
        [sds((ROWS, 128), jnp.int32)], [], 2 * ROWS * ROWS * 128, args,
    )[0]


def hot_rows(place_ref, count):
    columns = lax.broadcasted_iota(jnp.int32, (PADDED, count), 1)
    hit = (columns == place_ref[:, 0:1]) | (columns == place_ref[:, 1:2])
    return jnp.where(hit, 1.0, 0.0).astype(LOW)


def dispatch(places, rows, count):
    width = rows.shape[1]

    def body(place_ref, rows_ref, out_ref, acc):
        accumulate(acc, dot_tn(hot_rows(place_ref, count), rows_ref[...].astype(LOW)))

        @pl.when(pl.program_id(0) == SEQS - 1)
        def _():
            out_ref[...] = acc[...].astype(LOW)

    return call(
        body, "dispatch", (SEQS,), [wide(PADDED, 128), wide(PADDED, width)], [fixed((count, width))],
        [sds((count, width), LOW)], [pltpu.VMEM((count, width), FULL)], 2 * ROWS * count * width, [places, rows],
    )[0]


def mix_forward(entry, gain, shift, places, count):
    width = gain.shape[1]
    n_entry = len(entry)

    def body(*refs):
        gain_ref, shift_ref, place_ref = refs[n_entry : n_entry + 3]
        hid_ref, out0_ref, out1_ref, acc = refs[n_entry + 3 :]
        hidden = enter_forward(refs[:n_entry])
        hid_ref[...] = hidden
        low = (normalise(hidden)[0] * gain_ref[...] + shift_ref[...]).astype(LOW)
        accumulate(acc, dot_tn(hot_rows(place_ref, count), low))

        @pl.when(pl.program_id(0) == SEQS - 1)
        def _():
            out0_ref[...] = acc[: count // 2, :].astype(LOW)
            out1_ref[...] = acc[count // 2 :, :].astype(LOW)

    args = list(entry) + [gain, shift, places]
    in_specs = forward_specs(entry) + [fixed(gain.shape), fixed(shift.shape), wide(PADDED, 128)]
    out_shape = [sds((ROWS, width), FULL)] + [sds((count // 2, width), LOW)] * 2
    out_specs = [wide(PADDED, width)] + [fixed((count // 2, width))] * 2
    return call(
        body, "mix_forward", (SEQS,), in_specs, out_specs, out_shape, [pltpu.VMEM((count, width), FULL)],
        2 * ROWS * count * width, args,
    )


def combine(places, parts):
    count, width = sum(p.shape[0] for p in parts), parts[0].shape[1]

    def body(place_ref, *refs):
        hot = hot_rows(place_ref, count)
        rows = jnp.concatenate([r[...] for r in refs[:-1]], axis=0)
        refs[-1][...] = dot_nn(hot, rows).astype(LOW)

    return call(
        body, "combine", (SEQS,), [wide(PADDED, 128)] + [fixed(p.shape) for p in parts], [wide(PADDED, width)],
        [sds((ROWS, width), LOW)], [], 2 * ROWS * count * width, [places] + list(parts),
    )[0]


class Wires:
    def __init__(self):
        self.dp = lax.axis_size("dp")
        self.mp = lax.axis_size("mp")
        self.ring = self.dp // 2
        self.d = lax.axis_index("dp")
        self.m = lax.axis_index("mp")
        self.z = self.d // 2
        self.y = self.d % 2
        self.x = self.m // 2
        self.c = self.m % 2

    def move(self, value, to_d=lambda d: d, to_m=lambda m: m):
        pairs = [
            (d * self.mp + m, to_d(d) * self.mp + to_m(m)) for d in range(self.dp) for m in range(self.mp)
        ]
        return lax.ppermute(value, ("dp", "mp"), pairs)

    def swap_core(self, value):
        return self.move(value, to_m=lambda m: m ^ 1)

    def swap_x(self, value):
        return self.move(value, to_m=lambda m: m ^ 2)

    def swap_y(self, value):
        return self.move(value, to_d=lambda d: d ^ 1)

    def along_z(self, value):
        return self.move(value, to_d=lambda d: (d + 2) % self.dp)

    def swap_dp(self, value, step):
        return self.move(value, to_d=lambda d: d ^ step)

    def ring_pieces(self, shard):
        pieces, own = [], shard
        for step in range(self.ring):
            own = self.along_z(own) if step else own
            pieces += [own, self.swap_y(own)]
        return pieces

    def assemble(self, pieces):
        return assemble(jnp.stack([self.z, self.y]).astype(jnp.int32), pieces)

    def scatter(self, parts):
        rows, cols = parts.shape
        rows = rows // self.dp
        blocks = parts.reshape(self.ring, 2, rows, cols)
        away = lax.dynamic_index_in_dim(blocks, 1 - self.y, 1, keepdims=False).astype(LOW)
        stay = lax.dynamic_index_in_dim(blocks, self.y, 1, keepdims=False)
        arrived = self.swap_y(away)
        for step in range(self.ring):
            at = (self.z - 1 - step) % self.ring
            mine = lax.dynamic_index_in_dim(stay, at, 0, keepdims=False)
            mine = mine + lax.dynamic_index_in_dim(arrived, at, 0, keepdims=False).astype(FULL)
            total = mine if step == 0 else mine + self.along_z(total.astype(LOW)).astype(FULL)
        return total

    def scatter_x_first(self, own, peer):
        return self.scatter(own + self.swap_x(peer.astype(LOW)).astype(FULL))

    def scatter_x_last(self, own, peer):
        span = own.shape[1]
        whole = self.scatter(jnp.concatenate([own, peer], axis=1))
        return whole[:, :span] + self.swap_x(whole[:, span:].astype(LOW)).astype(FULL)

    def exchange(self, rows, portions=1):
        width = rows.shape[1]
        rows = rows.reshape(portions, self.dp, -1, width)
        rows = lax.all_to_all(rows, "dp", split_axis=1, concat_axis=1, tiled=True)
        return rows.reshape(-1, width)

    def total(self, value):
        value = value + self.swap_x(value)
        step = 1
        while step < self.dp:
            value = value + self.swap_dp(value, step)
            step *= 2
        return value


def after(value, done):
    return lax.optimization_barrier((value, done))[0]


def pad_rows(rows):
    width = rows.shape[1]
    rows = jnp.pad(rows.reshape(SEQS, SEQ, width), ((0, 0), (0, PADDED - SEQ), (0, 0)))
    return rows.reshape(ROWS, width)


def local(
    inputs, cotangent, ln_gain, ln_bias, w_qkv, b_qv, w_out, b_out, w_fc1, b_fc1, w_fc2, b_fc2,
    w_gate, e_in, e_in_bias, e_out, e_out_bias, routes,
):
    wires = Wires()
    width = inputs.shape[1]
    experts = w_gate.shape[1]
    capacity = ((MB_TOK * 2 * 5 // 4 + experts - 1) // experts + 7) // 8 * 8
    half = capacity // 2
    quota = (half + 1) // 2
    room = (quota + 15) // 16 * 16
    count = 2 * experts * room
    first = wires.x * MB_TOK
    span = w_out.shape[2]
    units = w_fc1.shape[1]

    def block_of(rows):
        return lax.dynamic_slice_in_dim(rows, first, MB_TOK, 0)

    def row_of(vector):
        return vector.reshape(1, -1)

    pack_shards = make_packs(w_qkv, w_out)
    pieces = wires.ring_pieces(jnp.concatenate([pack_shards[0], wires.swap_x(pack_shards[0])], axis=1))
    pack_whole = wires.assemble(pieces)
    pack0 = [(pack_whole, 0, 4 * span), (pack_whole, 1, 4 * span)]
    ring_end = pieces[-2]
    lanes = (experts + 127) // 128 * 128
    tail_shard = jnp.concatenate([pack_shards[1], jnp.pad(w_gate, ((0, 0), (0, lanes - experts)))], axis=1)
    tail_whole = lax.all_gather(after(tail_shard, ring_end), "dp", axis=0, tiled=True)
    up_pieces = wires.ring_pieces(after(w_fc1, ring_end))
    down_shard = jnp.concatenate([w_fc2, wires.swap_x(w_fc2)], axis=1)
    down_pieces = wires.ring_pieces(after(down_shard, up_pieces[-2]))
    up_own = wires.assemble(up_pieces)
    up_peer = wires.swap_x(up_own)
    up = [(up_own, 0, units), (up_peer, 0, units)]
    down_whole = wires.assemble(down_pieces)
    down = [(down_whole, 0, units), (down_whole, 1, units)]
    pack1_peer = wires.swap_x(tail_whole[:, : 4 * span])
    pack1 = [(tail_whole, 0, 4 * span), (pack1_peer, 0, 4 * span)]
    gate = (tail_whole, 4 * span // lanes, lanes)
    small = jnp.concatenate([b_qv.reshape(-1), b_fc1, e_in_bias.reshape(-1)])
    small_peer = wires.swap_x(small)
    n_qv = b_qv.size
    qv_bias = [s[:n_qv].reshape(b_qv.shape) for s in (small, small_peer)]
    up_bias = [row_of(s[n_qv : n_qv + units]) for s in (small, small_peer)]
    pair_bias = jnp.stack([row_of(s[n_qv + units :]) for s in (small, small_peer)])
    in_bias = jnp.concatenate([pair_bias, wires.swap_core(pair_bias)])

    cot = pad_rows(block_of(cotangent))
    route_rows = jnp.pad(pad_rows(block_of(routes) + 1) - 1, ((0, 0), (0, 126)), constant_values=-1)
    position = jnp.full((1, 128), wires.c, jnp.int32)
    places = place_rows(route_rows, position, experts, half, quota, room)
    g_rows = wires.exchange(after(dispatch(places, cot, count), down_pieces[-2]), 2)

    def quarter(own, done):
        own = after(own, done)
        peer = wires.swap_x(own)
        return [own, peer, wires.swap_core(own), wires.swap_core(peer)]

    out_pieces = quarter(e_out[0], up_peer)
    in_pieces = quarter(e_in[0], pack1_peer)

    def gain_of(l, k):
        return row_of(ln_gain[l, k])

    def shift_of(l, k):
        return row_of(ln_bias[l, k])

    hidden_in = pad_rows(block_of(inputs))
    hidden0, low0, qkv0, lse0, att0, part = attend_forward(
        [hidden_in], gain_of(0, 0), shift_of(0, 0), pack0, [b[0] for b in qv_bias]
    )
    entry = [hidden0, part, wires.swap_core(part), row_of(b_out[0])]
    hidden1, low1, acts, slopes, part = dense_forward(entry, gain_of(0, 1), shift_of(0, 1), up, up_bias, down)
    entry = [hidden1, part, wires.swap_core(part), row_of(b_fc2)]
    hidden2, low2, qkv1, lse1, att1, part = attend_forward(
        entry, gain_of(1, 0), shift_of(1, 0), pack1, [b[1] for b in qv_bias]
    )
    entry = [hidden2, part, wires.swap_core(part), row_of(b_out[1])]
    hidden3, *x_slots = mix_forward(entry, gain_of(1, 1), shift_of(1, 1), places, count)

    x_parts = [wires.exchange(x) for x in x_slots]
    ahead = expert_ahead(g_rows, out_pieces)
    named = (jnp.arange(lanes, dtype=jnp.int32) == wires.d).astype(FULL)[None, :]
    made = [
        expert_first(x, g_rows, ahead, i, in_pieces, in_bias, gate, e_out_bias, named, experts)
        for i, x in enumerate(x_parts)
    ]
    e_acts, e_pres, grad_x, e_weights, e_logs = zip(*made)
    back = [wires.exchange(gx) for gx in grad_x]
    result, keep, send, grad_eb, grad_ob, gate_part = expert_second(
        x_parts, g_rows, e_weights, e_logs, e_acts, e_pres, out_pieces, e_out_bias
    )
    part = combine(places, back)

    grad3, grad3_low, part, joined_own, joined_peer, sums3, bias3 = attend_backward(
        cot, part, wires.swap_core(part), hidden3, gain_of(1, 1), qkv1, lse1, pack1
    )
    result_back = wires.exchange(after(result, part), 2)
    gp1 = [
        jnp.concatenate([dot_tn(low2, j), dot_tn(grad3_low, att1[:, cut])], axis=1)
        for j, cut in ((joined_own, slice(0, span)), (joined_peer, slice(span, 2 * span)))
    ]
    grad2, grad2_low, part, pre_own, pre_peer, sums2, bias2 = dense_backward(
        grad3, part, wires.swap_core(part), hidden2, gain_of(1, 0), slopes, up, down
    )
    gd = [dot_tn(grad2_low, acts[:, :units]), dot_tn(grad2_low, acts[:, units:])]
    gu = [dot_tn(low1, pre_own), dot_tn(low1, pre_peer)]
    grad1, grad1_low, part, joined_own, joined_peer, sums1, bias1 = attend_backward(
        grad2, part, wires.swap_core(part), hidden1, gain_of(0, 1), qkv0, lse0, pack0
    )
    go0 = [dot_tn(grad1_low, att0[:, :span]), dot_tn(grad1_low, att0[:, span:])]
    gq0 = [dot_tn(low0, joined_own), dot_tn(low0, joined_peer)]
    grad0, sums0 = last_norm_back(grad1, part, wires.swap_core(part), hidden0, gain_of(0, 0))

    grad_pack1 = wires.scatter_x_last(*gp1)
    grad_fc2 = wires.scatter_x_first(*gd)
    grad_fc1 = wires.scatter_x_last(*gu)
    grad_out0 = wires.scatter_x_last(*go0)
    grad_qkv0 = wires.scatter_x_first(*gq0)
    pair_grads = keep + wires.swap_core(send).astype(FULL)
    expert_grads = pair_grads[0] + wires.swap_x(pair_grads[1].astype(LOW)).astype(FULL)
    eb = jnp.concatenate([grad_eb.reshape(4, units), grad_ob, jnp.zeros((3, units), FULL)])
    eb_other = wires.swap_core(eb)
    eb = jnp.concatenate([eb[:2] + eb_other[2:4], eb[4:] + eb_other[4:]])
    eb_other = wires.swap_x(eb)
    grad_in_bias = eb[0:1] + eb_other[1:2]
    grad_out_bias = eb[2:3] + eb_other[2:3]

    def whole_rows(block):
        there = wires.swap_x(block)
        top, low = jnp.where(wires.x == 0, block, there), jnp.where(wires.x == 0, there, block)
        return jnp.concatenate([top, low], axis=0)

    mixed = combine(places, [after(result_back, grad2)])
    outputs = whole_rows(last_hidden(hidden3, mixed, wires.swap_core(mixed)))
    grad_inputs = whole_rows(grad0).astype(FULL)

    def by_x(rows):
        return jnp.where(wires.x == 0, rows, rows[jnp.array([1, 0, 2, 3, 4, 5, 6, 7])])

    gate_rows = gate_part[: (experts + 7) // 8 * 8]
    gate_rows = gate_rows + wires.swap_core(gate_rows)
    early = wires.total(jnp.concatenate([sums3, sums2, by_x(bias3), by_x(bias2), gate_rows]))
    late = wires.total(jnp.concatenate([sums1, sums0, by_x(bias1)]))
    grad_gain = jnp.stack([late[8], late[0], early[8], early[0]]).reshape(2, 2, width)
    grad_shift = jnp.stack([late[9], late[1], early[9], early[1]]).reshape(2, 2, width)
    grad_bout = jnp.stack([late[2], early[2]])

    def pick(rows):
        return lax.dynamic_index_in_dim(rows, wires.x, 0, keepdims=False)

    def qv_of(row):
        return jnp.stack([row[:span], row[2 * span : 3 * span]])

    grad_qv = jnp.stack([qv_of(pick(late[16:18])), qv_of(pick(early[16:18]))])
    grad_up_bias = pick(early[24:26])
    shard = w_gate.shape[0]
    grad_gate = lax.dynamic_slice_in_dim(early[32 : 32 + experts], wires.d * shard, shard, 1).T
    grad_qkv = jnp.stack([grad_qkv0, grad_pack1[:, : 3 * span]]).reshape(w_qkv.shape)
    grad_out = jnp.stack([grad_out0, grad_pack1[:, 3 * span :]])
    return (
        outputs,
        grad_inputs,
        grad_gain,
        grad_shift,
        grad_qkv,
        grad_qv,
        grad_out,
        grad_bout,
        grad_fc1,
        grad_up_bias,
        grad_fc2,
        early[10],
        grad_gate,
        expert_grads[0][None],
        grad_in_bias,
        expert_grads[1][None],
        grad_out_bias,
    )


def solution(mesh):
    in_specs = (
        P("dp", None), P("dp", None), P(), P(), P(None, "dp", None, "mp"), P(None, None, "mp"),
        P(None, "dp", "mp"), P(), P("dp", "mp"), P("mp"), P("dp", "mp"), P(), P("dp", None),
        P("dp", None, "mp"), P("dp", "mp"), P("dp", None, "mp"), P("dp", None), P("dp", None),
    )
    out_specs = (
        P("dp", None), P("dp", None), P(), P(), P(None, "dp", None, "mp"), P(None, None, "mp"),
        P(None, "dp", "mp"), P(), P("dp", "mp"), P("mp"), P("dp", "mp"), P(), P("dp", None),
        P("dp", None, "mp"), P("dp", "mp"), P("dp", None, "mp"), P("dp", None),
    )
    return jax.shard_map(local, mesh=mesh, in_specs=in_specs, out_specs=out_specs, check_vma=False)
```
